32 devices in a mesh: pipe: 2 (over core), ctx: 16 (over z, y, x).
Axes of the slice: x: 2, y: 2, z: 4, core: 2. Of those that a mesh axis runs over, the one named last changes fastest.
Arguments:
- arriving: bfloat16 [2, 4096, 2048], P('pipe', None, 'ctx'), may hold values from -6 to 6
- input_gate: bfloat16 [2, 4096, 2048], P('pipe', None, 'ctx'), may hold values from -6 to 6
- input_inner: bfloat16 [2, 4096, 2048], P('pipe', None, 'ctx'), may hold values from -6 to 6
- values: bfloat16 [2, 4096, 2048], P('pipe', None, 'ctx'), may hold values from -6 to 6
- conv_out: bfloat16 [2, 4096, 2048], P('pipe', None, 'ctx'), may hold values from -6 to 6
- filters: bfloat16 [2, 4096, 2048], P('pipe', None, 'ctx'), may hold values from -1 to 1
- bias: float32 [2, 4096], P('pipe'), may hold values from 0.5 to 1.5
Outputs:
- d_gate: bfloat16 [2, 4096, 2048], P('pipe', None, 'ctx')
- inner_gradient: bfloat16 [2, 4096, 2048], P('pipe', None, 'ctx')
- d_values: bfloat16 [2, 4096, 2048], P('pipe', None, 'ctx')
- d_filters: float32 [2, 4096, 2048], P('pipe', None, 'ctx')
The draws below stay inside these ranges and needn't reach their ends.
All inputs are finite; a program needn't handle non-finite values.
Results may differ from the reference program's by a relative error of at most 0.011.
Values may be sent and summed in bfloat16 or wider, within the bound.
A program may use at most 128 MiB of HBM per device.

```python
import math
import jax
import jax.numpy as jnp
from jax import lax

C = 4096
TOK_DEV = 128
TOKEN_COUNT = 2048
HANDOFF_LAYERS = 2
N_CTX = 16


def draw_filters(key, part):
    key_rate = jax.random.fold_in(key, 11)
    key_taps = jax.random.fold_in(key, 12)
    cluster_seed_state = jax.random.fold_in(key, 13)
    low = math.log(0.1 / TOKEN_COUNT)
    high = math.log(1.0 / 40.0)
    rate = jnp.exp(jax.random.uniform(key_rate, (HANDOFF_LAYERS, C, 1), jnp.float32, low, high))
    steps = jnp.arange(TOKEN_COUNT, dtype=jnp.float32)[None, None, :]
    batch_clusters = jax.random.randint(cluster_seed_state, (HANDOFF_LAYERS, 3, 1), 1, TOKEN_COUNT)
    forwarded_message = jnp.sum((jnp.arange(TOKEN_COUNT, dtype=jnp.int32)[None, None, :] >= batch_clusters).astype(jnp.float32), axis=1, keepdims=True)
    envelope = jnp.exp(-rate * steps) * jnp.power(jnp.float32(0.7), forwarded_message)
    noise = jnp.clip(jax.random.normal(key_taps, (HANDOFF_LAYERS, C, TOKEN_COUNT), jnp.float32), -4.0, 4.0)
    taps = noise * envelope * jnp.sqrt(2.0 * rate + 1.0 / TOKEN_COUNT)
    return taps.astype(jnp.bfloat16)


def block_scale(stream_key, dims, shards, smallest, largest):
    factor_of = 1.0
    for position, shards_of in shards:
        steps = jax.random.uniform(jax.random.fold_in(jax.random.fold_in(stream_key, 6), position), (shards_of,), jnp.float32, smallest / len(shards), largest / len(shards))
        factor_of = factor_of * jnp.repeat(jnp.exp(steps), dims[position] // shards_of).reshape((-1,) + (1,) * (len(dims) - 1 - position))
    return factor_of


def gaussian(key, extent, scale, limit, cuts=(), kind=jnp.bfloat16):
    gain = block_scale(key, extent, cuts, -0.22, 0.18) if cuts else 1.0
    values = jax.random.normal(key, extent, jnp.float32) * scale * gain
    return jnp.minimum(jnp.maximum(values, -limit), limit).astype(kind)


def setup_inputs(seed: int = 0) -> dict:
    key_of = jax.random.split(jax.random.key(seed), 8)
    arriving = gaussian(key_of[0], (HANDOFF_LAYERS, C, TOKEN_COUNT), 1.0, 6.0, ((0, 2), (2, 16)))
    input_gate = gaussian(key_of[1], (HANDOFF_LAYERS, C, TOKEN_COUNT), 1.0, 6.0, ((0, 2), (2, 16)))
    input_inner = gaussian(key_of[2], (HANDOFF_LAYERS, C, TOKEN_COUNT), 1.0, 6.0, ((0, 2), (2, 16)))
    values = gaussian(key_of[3], (HANDOFF_LAYERS, C, TOKEN_COUNT), 1.0, 6.0, ((0, 2), (2, 16)))
    conv_out = gaussian(key_of[4], (HANDOFF_LAYERS, C, TOKEN_COUNT), 1.0, 6.0, ((0, 2), (2, 16)))
    filters = draw_filters(jax.random.fold_in(key_of[7], 71), 0)
    bias = jnp.clip(0.5 + 1.0 * jax.random.uniform(key_of[6], (HANDOFF_LAYERS, C), jnp.float32) ** block_scale(key_of[6], (HANDOFF_LAYERS, C), ((0, 2),), -0.2, 0.2), 0.5, 1.5)
    return dict(arriving=arriving, input_gate=input_gate, input_inner=input_inner, values=values, conv_out=conv_out, filters=filters, bias=bias)


def angle_table(rows, cols, period, row_start, col_start):
    left = (jnp.arange(rows, dtype=jnp.int32) + row_start)[:, None]
    right = (jnp.arange(cols, dtype=jnp.int32) + col_start)[None, :]
    phase = (left * right % period).astype(jnp.float32) * (2.0 * math.pi / period)
    return (jnp.cos(phase), jnp.sin(phase))

def rounded(value):
    return lax.optimization_barrier(value.astype(jnp.bfloat16)).astype(jnp.float32)

def contract(form, left, right):
    return jnp.einsum(form, left, right, precision=lax.Precision.HIGHEST)

def section_block(tiles_list, tokens_dev, tables, pieces):
    cos_a, sin_a, cos_b, sin_b, cos_w, sin_w = tables
    other, gate_in, inner_in, values, saved, taps, bias = pieces
    channel_count = other.shape[0]
    seq_length = tiles_list * tokens_dev
    inner = (inner_in.astype(jnp.float32) * values.astype(jnp.float32)).astype(jnp.bfloat16)
    d_out = (other.astype(jnp.float32) * gate_in.astype(jnp.float32)).astype(jnp.bfloat16)
    d_gate = (other.astype(jnp.float32) * saved.astype(jnp.float32)).astype(jnp.bfloat16)

    def forward(signal):
        columns = signal.astype(jnp.float32).reshape(channel_count, tiles_list, tokens_dev)
        real_sum = contract('caj,ak->cjk', columns, cos_a)
        imag_sum = -contract('caj,ak->cjk', columns, sin_a)
        part_real = rounded(real_sum * cos_w + imag_sum * sin_w)
        part_imag = rounded(imag_sum * cos_w - real_sum * sin_w)
        spec_real = contract('cjk,jm->ckm', part_real, cos_b) + contract('cjk,jm->ckm', part_imag, sin_b)
        spec_imag = contract('cjk,jm->ckm', part_imag, cos_b) - contract('cjk,jm->ckm', part_real, sin_b)
        return (rounded(spec_real), rounded(spec_imag))
    z_real, latent_quadrature = forward(inner)
    h_real, h_imag = forward(taps)
    d_real, d_imag = forward(d_out)
    shrink = 1.0 / math.sqrt(seq_length)
    z_real = z_real * shrink
    latent_quadrature = latent_quadrature * shrink
    q_real = rounded(h_real * d_real + h_imag * d_imag - (z_real * d_imag - latent_quadrature * d_real))
    q_imag = rounded(h_real * d_imag - h_imag * d_real + z_real * d_real + latent_quadrature * d_imag)
    even_real = contract('ckm,jm->ckj', q_real, cos_b) - contract('ckm,jm->ckj', q_imag, sin_b)
    even_imag = contract('ckm,jm->ckj', q_imag, cos_b) + contract('ckm,jm->ckj', q_real, sin_b)
    twist_cos = cos_w.T
    rotation_sine = sin_w.T
    back_real = rounded(even_real * twist_cos - even_imag * rotation_sine)
    back_imag = rounded(even_real * rotation_sine + even_imag * twist_cos)
    scale = 1.0 / (2 * seq_length)
    out_real = (contract('ckj,ak->caj', back_real, cos_a) - contract('ckj,ak->caj', back_imag, sin_a)) * scale
    out_imag = (contract('ckj,ak->caj', back_imag, cos_a) + contract('ckj,ak->caj', back_real, sin_a)) * scale
    gradient_inner_part = out_real.reshape(channel_count, seq_length) + bias[:, None] * d_out.astype(jnp.float32)
    d_taps = out_imag.reshape(channel_count, seq_length)
    inner_gradient = (gradient_inner_part * values.astype(jnp.float32)).astype(jnp.bfloat16)
    d_values = (gradient_inner_part * inner_in.astype(jnp.float32)).astype(jnp.bfloat16)
    return (d_gate, inner_gradient, d_values, d_taps)

def reference(arriving, input_gate, input_inner, values, conv_out, filters, bias):
    tiles_list = N_CTX
    tokens_dev = TOK_DEV
    full_length = 2 * tiles_list * tokens_dev
    cos_a, sin_a = angle_table(tiles_list, 2 * tiles_list, 2 * tiles_list, 0, 0)
    cos_b, sin_b = angle_table(tokens_dev, tokens_dev, tokens_dev, 0, 0)
    cos_w, sin_w = angle_table(tokens_dev, 2 * tiles_list, full_length, 0, 0)
    tables = (cos_a.astype(jnp.bfloat16).astype(jnp.float32), sin_a.astype(jnp.bfloat16).astype(jnp.float32), cos_b.astype(jnp.bfloat16).astype(jnp.float32), sin_b.astype(jnp.bfloat16).astype(jnp.float32), cos_w, sin_w)
    block_width = math.gcd(C, 256)
    block_count = C // block_width
    results = []
    for section in range(HANDOFF_LAYERS):

        def split_rows(array):
            return array.reshape(block_count, block_width, TOKEN_COUNT)
        pieces = (split_rows(arriving[(section + 1) % HANDOFF_LAYERS]), split_rows(input_gate[section]), split_rows(input_inner[section]), split_rows(values[section]), split_rows(conv_out[section]), split_rows(filters[section]), bias[section].reshape(block_count, block_width))
        mapped = lax.map(partial_block(tiles_list, tokens_dev, tables), pieces)
        results.append([entry.reshape(C, TOKEN_COUNT) for entry in mapped])
    return (jnp.stack([entry[0] for entry in results]), jnp.stack([entry[1] for entry in results]), jnp.stack([entry[2] for entry in results]), jnp.stack([entry[3] for entry in results]))

def partial_block(tiles_list, tokens_dev, tables):

    def apply_block(pieces):
        return section_block(tiles_list, tokens_dev, tables, pieces)
    return apply_block
```

```python
import functools
import math

import jax
import jax.numpy as jnp
import numpy as np
from jax import lax
from jax.experimental import pallas as pl
from jax.experimental.pallas import tpu as pltpu
from jax.sharding import PartitionSpec as P


def plus(a, b):
    return b if a is None else a if b is None else a + b


def minus(a, b):
    return a if b is None else -b if a is None else a - b


def turn(a, b, k, n):
    k = k % n
    if k == 0:
        return a, b
    if 4 * k == n:
        return b, minus(None, a)
    if 4 * k == 3 * n:
        return minus(None, b), a
    c, s = math.cos(2 * math.pi * k / n), math.sin(2 * math.pi * k / n)

    def scaled(v, f):
        return None if v is None else v * f

    if 8 * k == n:
        return scaled(plus(a, b), c), scaled(minus(b, a), c)
    return plus(scaled(a, c), scaled(b, s)), minus(scaled(b, c), scaled(a, s))


def real_dft(x, n):
    if n == 2:
        return [(x[0], None), (x[0], None)]
    even, odd = real_dft(x[0::2], n // 2), real_dft(x[1::2], n // 2)
    out = [None] * (n // 2 + 1)
    for k in range(n // 4 + 1):
        er, ei = even[k]
        tr, ti = turn(*odd[k], k, n)
        if 4 * k == n:
            out[k] = (plus(er, tr), plus(ei, ti))
        else:
            out[k] = (plus(er, tr), plus(ei, ti))
            out[n // 2 - k] = (minus(er, tr), minus(ti, ei))
    return out


def real_inverse(spec, n):
    if n == 2:
        return [plus(spec[0][0], spec[1][0])]
    even, odd = [], []
    for k in range(n // 4 + 1):
        xr, xi = spec[k]
        if 4 * k == n:
            even.append((xr + xr, None))
            odd.append((minus(None, None if xi is None else xi + xi), None))
            continue
        yr, yi = spec[n // 2 - k]
        even.append((plus(xr, yr), minus(xi, yi)))
        dr, di = minus(xr, yr), plus(xi, yi)
        odd.append(turn(dr, di, -k, n))
    even[0], odd[0] = (even[0][0], None), (odd[0][0], None)
    first, second = real_inverse(even, n // 2), real_inverse(odd, n // 2)
    return [v for pair in zip(first, second) for v in pair]


def tables(tiles, tokens):
    full = 2 * tiles * tokens
    j = np.arange(tokens)
    phase = 2 * np.pi * ((j[:, None] * j[None, :]) % tokens) / tokens
    cb, sb = np.cos(phase), np.sin(phase)
    forward = np.block([[cb, -sb], [sb, cb]])
    k = np.arange(tiles + 1)
    angle = 2 * np.pi * ((k[:, None] * j[None, :]) % full) / full
    twist = np.stack([np.cos(angle), np.sin(angle)], axis=1)
    return (
        jnp.asarray(forward, jnp.bfloat16),
        jnp.asarray(forward.T, jnp.bfloat16),
        jnp.asarray(twist, jnp.float32),
    )


ROWS = 16


def transform(rx, out, w, wi, twist, spec, back):
    _, tiles, rows, tokens = rx.shape
    full = 2 * tiles * tokens
    shrink = 1.0 / math.sqrt(tiles * tokens)
    steps = rows // ROWS

    def first(t, carry):
        s, i = t // steps, t % steps
        at = pl.ds(pl.multiple_of(i * ROWS, ROWS), ROWS)
        x = [rx[s, a, at, :].astype(jnp.float32) for a in range(tiles)]
        for k, (re, im) in enumerate(real_dft(x, 2 * tiles)):
            if k == 0:
                new_re, new_im = re, jnp.zeros_like(re)
            else:
                c, d = twist[k, 0:1, :], twist[k, 1:2, :]
                new_re = plus(re * c, None if im is None else im * d)
                new_im = minus(None if im is None else im * c, re * d)
            spec[s, k, at, 0:tokens] = new_re.astype(jnp.bfloat16)
            spec[s, k, at, tokens : 2 * tokens] = new_im.astype(jnp.bfloat16)
        return carry

    lax.fori_loop(0, 3 * steps, first, 0)

    def middle(k, carry):
        def spectrum(s):
            u = jnp.dot(spec[s, k], w[...], preferred_element_type=jnp.float32)
            u = u.astype(jnp.bfloat16).astype(jnp.float32)
            return u[:, :tokens], u[:, tokens:]

        hr, hi = spectrum(0)
        zr, zi = spectrum(1)
        dr, di = spectrum(2)
        c = twist[k, 0:1, :] * (1.0 / full)
        d = twist[k, 1:2, :] * (1.0 / full)
        for s, (ur, ui, f) in enumerate(((hr, hi, 1.0), (zr, zi, shrink))):
            qr = ur * dr + ui * di
            qi = ur * di - ui * dr
            if s:
                qr, qi = qr * f, qi * f
            q = jnp.concatenate([qr, qi], axis=1).astype(jnp.bfloat16)
            e = jnp.dot(q, wi[...], preferred_element_type=jnp.float32)
            er, ei = e[:, :tokens], e[:, tokens:]
            back[s, k, :, 0:tokens] = (er * c - ei * d).astype(jnp.bfloat16)
            back[s, k, :, tokens : 2 * tokens] = (er * d + ei * c).astype(jnp.bfloat16)
        return carry

    lax.fori_loop(0, tiles + 1, middle, 0)

    def last(t, carry):
        s, i = t // steps, t % steps
        at = pl.ds(pl.multiple_of(i * ROWS, ROWS), ROWS)
        pieces = []
        for k in range(tiles + 1):
            re = back[s, k, at, 0:tokens].astype(jnp.float32)
            im = None
            if 0 < k < tiles:
                im = back[s, k, at, tokens : 2 * tokens].astype(jnp.float32)
            pieces.append((re, im))
        for a, value in enumerate(real_inverse(pieces, 2 * tiles)):
            out[s, a, at, :] = value.astype(jnp.bfloat16)
        return carry

    lax.fori_loop(0, 2 * steps, last, 0)


def local_call(received):
    _, tiles, own, tokens = received.shape
    w, wi, twist = tables(tiles, tokens)

    def body(rx, w_ref, wi_ref, twist_ref, out, spec, back):
        transform(rx, out, w_ref, wi_ref, twist_ref, spec, back)

    group = max(ROWS, own // 4)

    def whole(shape):
        return pl.BlockSpec(shape, lambda g: (0,) * len(shape))

    return pl.pallas_call(
        body,
        grid=(own // group,),
        in_specs=[
            pl.BlockSpec((3, tiles, group, tokens), lambda g: (0, 0, g, 0)),
            whole(w.shape),
            whole(wi.shape),
            whole(twist.shape),
        ],
        out_specs=pl.BlockSpec((2, tiles, group, tokens), lambda g: (0, 0, g, 0)),
        out_shape=jax.ShapeDtypeStruct((2, tiles, own, tokens), jnp.bfloat16),
        scratch_shapes=[
            pltpu.VMEM((3, tiles + 1, group, 2 * tokens), jnp.bfloat16),
            pltpu.VMEM((2, tiles + 1, group, 2 * tokens), jnp.bfloat16),
        ],
        compiler_params=pltpu.CompilerParams(vmem_limit_bytes=56 * 2**20),
    )(received, w, wi, twist)


def per_device(arriving, input_gate, input_inner, values, conv_out, filters, bias):
    tiles = lax.axis_size("ctx")
    sections = lax.axis_size("pipe")
    channels, tokens = values.shape[1:]
    own = channels // tiles
    f32, bf16 = jnp.float32, jnp.bfloat16
    route = [((i + 1) % sections, i) for i in range(sections)]
    grad = lax.ppermute(arriving[0], "pipe", route).astype(f32)
    inner_in, vals = input_inner[0].astype(f32), values[0].astype(f32)
    inner = (inner_in * vals).astype(bf16)
    d_out = (grad * input_gate[0].astype(f32)).astype(bf16)
    d_gate = (grad * conv_out[0].astype(f32)).astype(bf16)
    sent = jnp.stack([filters[0], inner, d_out]).reshape(3, tiles, own, tokens)
    received = lax.all_to_all(sent, "ctx", split_axis=1, concat_axis=1, tiled=True)
    result = local_call(received)
    q = lax.all_to_all(result, "ctx", split_axis=1, concat_axis=1, tiled=True)
    q = q.reshape(2, channels, tokens).astype(f32)
    dz = q[0] + bias[0][:, None] * d_out.astype(f32)
    inner_gradient = (dz * vals).astype(bf16)
    d_values = (dz * inner_in).astype(bf16)
    return (d_gate[None], inner_gradient[None], d_values[None], q[1][None])


def solution(mesh):
    spread = P("pipe", None, "ctx")
    return jax.shard_map(
        per_device,
        mesh=mesh,
        in_specs=(spread,) * 6 + (P("pipe", None),),
        out_specs=(spread,) * 4,
        check_vma=False,
    )
```

```python
import functools
import math

import jax
import jax.numpy as jnp
import numpy as np
from jax import lax
from jax.experimental import pallas as pl
from jax.experimental.pallas import tpu as pltpu
from jax.sharding import PartitionSpec as P


def plus(a, b):
    return b if a is None else a if b is None else a + b


def minus(a, b):
    return a if b is None else -b if a is None else a - b


def turn(a, b, k, n):
    k = k % n
    if k == 0:
        return a, b
    if 4 * k == n:
        return b, minus(None, a)
    if 4 * k == 3 * n:
        return minus(None, b), a
    c, s = math.cos(2 * math.pi * k / n), math.sin(2 * math.pi * k / n)

    def scaled(v, f):
        return None if v is None else v * f

    if 8 * k == n:
        return scaled(plus(a, b), c), scaled(minus(b, a), c)
    return plus(scaled(a, c), scaled(b, s)), minus(scaled(b, c), scaled(a, s))


def real_dft(x, n):
    if n == 2:
        return [(x[0], None), (x[0], None)]
    even, odd = real_dft(x[0::2], n // 2), real_dft(x[1::2], n // 2)
    out = [None] * (n // 2 + 1)
    for k in range(n // 4 + 1):
        er, ei = even[k]
        tr, ti = turn(*odd[k], k, n)
        if 4 * k == n:
            out[k] = (plus(er, tr), plus(ei, ti))
        else:
            out[k] = (plus(er, tr), plus(ei, ti))
            out[n // 2 - k] = (minus(er, tr), minus(ti, ei))
    return out


def real_inverse(spec, n):
    if n == 2:
        return [plus(spec[0][0], spec[1][0])]
    even, odd = [], []
    for k in range(n // 4 + 1):
        xr, xi = spec[k]
        if 4 * k == n:
            even.append((xr + xr, None))
            odd.append((minus(None, None if xi is None else xi + xi), None))
            continue
        yr, yi = spec[n // 2 - k]
        even.append((plus(xr, yr), minus(xi, yi)))
        dr, di = minus(xr, yr), plus(xi, yi)
        odd.append(turn(dr, di, -k, n))
    even[0], odd[0] = (even[0][0], None), (odd[0][0], None)
    first, second = real_inverse(even, n // 2), real_inverse(odd, n // 2)
    return [v for pair in zip(first, second) for v in pair]


def tables(tiles, tokens):
    full = 2 * tiles * tokens
    j = np.arange(tokens)
    phase = 2 * np.pi * ((j[:, None] * j[None, :]) % tokens) / tokens
    cb, sb = np.cos(phase), np.sin(phase)
    forward = np.block([[cb, -sb], [sb, cb]])
    k = np.arange(tiles + 1)
    angle = 2 * np.pi * ((k[:, None] * j[None, :]) % full) / full
    twist = np.stack([np.cos(angle), np.sin(angle)], axis=1)
    return (
        jnp.asarray(forward, jnp.bfloat16),
        jnp.asarray(forward.T, jnp.bfloat16),
        jnp.asarray(twist, jnp.float32),
    )


ROWS = 16


def transform(rx, out, w, wi, twist, spec, back):
    _, tiles, rows, tokens = rx.shape
    full = 2 * tiles * tokens
    shrink = 1.0 / math.sqrt(tiles * tokens)
    steps = rows // ROWS

    def first(t, carry):
        s, i = lax.div(t, steps), lax.rem(t, steps)
        at = pl.ds(pl.multiple_of(i * ROWS, ROWS), ROWS)
        x = [rx[s, a, at, :].astype(jnp.float32) for a in range(tiles)]
        for k, (re, im) in enumerate(real_dft(x, 2 * tiles)):
            if k == 0:
                new_re, new_im = re, jnp.zeros_like(re)
            else:
                c, d = twist[k, 0:1, :], twist[k, 1:2, :]
                new_re = plus(re * c, None if im is None else im * d)
                new_im = minus(None if im is None else im * c, re * d)
            spec[s, k, at, 0:tokens] = new_re.astype(jnp.bfloat16)
            spec[s, k, at, tokens : 2 * tokens] = new_im.astype(jnp.bfloat16)
        return carry

    lax.fori_loop(0, 3 * steps, first, 0)

    def middle(k, carry):
        def spectrum(s):
            u = jnp.dot(spec[s, k], w[...], preferred_element_type=jnp.float32)
            u = u.astype(jnp.bfloat16).astype(jnp.float32)
            return u[:, :tokens], u[:, tokens:]

        hr, hi = spectrum(0)
        zr, zi = spectrum(1)
        dr, di = spectrum(2)
        c = twist[k, 0:1, :] * (1.0 / full)
        d = twist[k, 1:2, :] * (1.0 / full)
        for s, (ur, ui, f) in enumerate(((hr, hi, 1.0), (zr, zi, shrink))):
            qr = ur * dr + ui * di
            qi = ur * di - ui * dr
            if s:
                qr, qi = qr * f, qi * f
            q = jnp.concatenate([qr, qi], axis=1).astype(jnp.bfloat16)
            e = jnp.dot(q, wi[...], preferred_element_type=jnp.float32)
            er, ei = e[:, :tokens], e[:, tokens:]
            back[s, k, :, 0:tokens] = (er * c - ei * d).astype(jnp.bfloat16)
            back[s, k, :, tokens : 2 * tokens] = (er * d + ei * c).astype(jnp.bfloat16)
        return carry

    lax.fori_loop(0, tiles + 1, middle, 0)

    def last(t, carry):
        s, i = lax.div(t, steps), lax.rem(t, steps)
        at = pl.ds(pl.multiple_of(i * ROWS, ROWS), ROWS)
        pieces = []
        for k in range(tiles + 1):
            re = back[s, k, at, 0:tokens].astype(jnp.float32)
            im = None
            if 0 < k < tiles:
                im = back[s, k, at, tokens : 2 * tokens].astype(jnp.float32)
            pieces.append((re, im))
        for a, value in enumerate(real_inverse(pieces, 2 * tiles)):
            out[s, a, at, :] = value.astype(jnp.bfloat16)
        return carry

    lax.fori_loop(0, 2 * steps, last, 0)


MESH = pl.DeviceIdType.MESH


def kernel(
    n, sections, group,
    arriving, taps, gate, inner_in, vals, w, wi, twist,
    grad_out, q,
    grad, stage, rx, res, spec, back,
    pair_send, pair_recv, send, recv, home, back_send, back_recv, back_home, grad_home,
):
    me, sec = lax.axis_index("ctx"), lax.axis_index("pipe")
    groups = arriving.shape[1] // group

    def rows_of(g):
        return pl.ds(pl.multiple_of(g * group, group), group)

    def peer_of(d):
        return lax.rem(me + d, n)

    barrier = pltpu.get_barrier_semaphore()
    pl.semaphore_signal(
        barrier, inc=1, device_id={"pipe": lax.rem(sec + 1, sections)}, device_id_type=MESH
    )

    def greet(d, carry):
        pl.semaphore_signal(barrier, inc=1, device_id={"ctx": peer_of(d)}, device_id_type=MESH)
        return carry

    lax.fori_loop(1, n, greet, 0)
    pl.semaphore_wait(barrier, n)

    def pair(g):
        return pltpu.make_async_remote_copy(
            src_ref=arriving.at[:, rows_of(g)],
            dst_ref=grad.at[:, rows_of(g)],
            send_sem=pair_send.at[g],
            recv_sem=pair_recv.at[g],
            device_id={"pipe": lax.rem(sec + sections - 1, sections)},
            device_id_type=MESH,
        )

    def start_pair(g, carry):
        pair(g).start()
        return carry

    lax.fori_loop(0, groups, start_pair, 0)

    def ship(src, g, s, p):
        pltpu.make_async_remote_copy(
            src_ref=src,
            dst_ref=rx.at[g, s, me],
            send_sem=send.at[g],
            recv_sem=recv.at[g],
            device_id={"ctx": p},
            device_id_type=MESH,
        ).start()

    def own_taps(g):
        return pltpu.make_async_copy(taps.at[me, rows_of(g)], rx.at[g, 0, me], home.at[g])

    def keep_grad(g):
        return pltpu.make_async_copy(
            grad.at[:, rows_of(g)], grad_out.at[:, rows_of(g)], grad_home.at[g]
        )

    def forward(g, carry):
        rows = rows_of(g)

        def send_taps(d, c):
            ship(taps.at[peer_of(d), rows], g, 0, peer_of(d))
            return c

        lax.fori_loop(1, n, send_taps, 0)
        own_taps(g).start()

        def product(left, right, s):
            def one(p):
                return (left[p, rows].astype(jnp.float32) * right[p, rows].astype(jnp.float32)).astype(
                    jnp.bfloat16
                )

            def make(d, c):
                stage[g, s - 1, peer_of(d)] = one(peer_of(d))
                return c

            lax.fori_loop(1, n, make, 0)
            rx[g, s, me] = one(me)

            def post(d, c):
                ship(stage.at[g, s - 1, peer_of(d)], g, s, peer_of(d))
                return c

            lax.fori_loop(1, n, post, 0)

        product(inner_in, vals, 1)
        pair(g).wait_recv()
        keep_grad(g).start()
        product(grad, gate, 2)
        return carry

    lax.fori_loop(0, groups, forward, 0)

    def own_result(g):
        return pltpu.make_async_copy(
            res.at[g, :, me], q.at[:, me, rows_of(g)], back_home.at[g]
        )

    def turn_group(g, carry):
        landed = rx.at[g, :, pl.ds(0, n - 1)]
        pltpu.make_async_copy(landed, landed, recv.at[g]).wait()
        own_taps(g).wait()
        transform(rx.at[g], res.at[g], w, wi, twist, spec, back)

        def reply(d, c):
            pltpu.make_async_remote_copy(
                src_ref=res.at[g, :, peer_of(d)],
                dst_ref=q.at[:, me, rows_of(g)],
                send_sem=back_send.at[g],
                recv_sem=back_recv.at[0],
                device_id={"ctx": peer_of(d)},
                device_id_type=MESH,
            ).start()
            return c

        lax.fori_loop(1, n, reply, 0)
        own_result(g).start()
        return carry

    lax.fori_loop(0, groups, turn_group, 0)

    def finish(g, carry):
        pair(g).wait_send()
        keep_grad(g).wait()
        own_result(g).wait()
        sent = rx.at[g, :, pl.ds(0, n - 1)]
        pltpu.make_async_copy(sent, sent, send.at[g]).wait()
        replied = res.at[g, :, pl.ds(0, n - 1)]
        pltpu.make_async_copy(replied, replied, back_send.at[g]).wait()
        return carry

    lax.fori_loop(0, groups, finish, 0)
    everything = q.at[:, pl.ds(0, n - 1)]
    pltpu.make_async_copy(everything, everything, back_recv.at[0]).wait()


def exchange(arriving, taps, gate, inner_in, vals, n, sections):
    _, own, tokens = arriving.shape
    group = max(ROWS, own // 4)
    groups = own // group
    w, wi, twist = tables(n, tokens)
    bf16 = jnp.bfloat16
    vmem = pl.BlockSpec(memory_space=pltpu.VMEM)
    hbm = pl.BlockSpec(memory_space=pl.ANY)
    dma = pltpu.SemaphoreType.DMA
    return pl.pallas_call(
        functools.partial(kernel, n, sections, group),
        in_specs=[hbm, hbm, vmem, vmem, vmem, vmem, vmem, vmem],
        out_specs=[hbm, hbm],
        out_shape=[
            jax.ShapeDtypeStruct((n, own, tokens), bf16),
            jax.ShapeDtypeStruct((2, n, own, tokens), bf16),
        ],
        scratch_shapes=[
            pltpu.VMEM((n, own, tokens), bf16),
            pltpu.VMEM((groups, 2, n, group, tokens), bf16),
            pltpu.VMEM((groups, 3, n, group, tokens), bf16),
            pltpu.VMEM((groups, 2, n, group, tokens), bf16),
            pltpu.VMEM((3, n + 1, group, 2 * tokens), bf16),
            pltpu.VMEM((2, n + 1, group, 2 * tokens), bf16),
            dma((groups,)), dma((groups,)), dma((groups,)), dma((groups,)), dma((groups,)),
            dma((groups,)), dma((1,)), dma((groups,)), dma((groups,)),
        ],
        compiler_params=pltpu.CompilerParams(
            collective_id=0, has_side_effects=True, vmem_limit_bytes=56 * 2**20
        ),
    )(arriving, taps, gate, inner_in, vals, w, wi, twist)


def per_device(arriving, input_gate, input_inner, values, conv_out, filters, bias):
    tiles = lax.axis_size("ctx")
    sections = lax.axis_size("pipe")
    channels, tokens = values.shape[1:]
    own = channels // tiles
    f32, bf16 = jnp.float32, jnp.bfloat16

    def split(array):
        return array[0].reshape(tiles, own, tokens)

    grad, q = exchange(
        split(arriving), split(filters), split(input_gate), split(input_inner), split(values),
        tiles, sections,
    )
    grad = grad.reshape(channels, tokens).astype(f32)
    q = q.reshape(2, channels, tokens).astype(f32)
    d_out = (grad * input_gate[0].astype(f32)).astype(bf16).astype(f32)
    d_gate = (grad * conv_out[0].astype(f32)).astype(bf16)
    dz = q[0] + bias[0][:, None] * d_out
    inner_gradient = (dz * values[0].astype(f32)).astype(bf16)
    d_values = (dz * input_inner[0].astype(f32)).astype(bf16)
    return (d_gate[None], inner_gradient[None], d_values[None], q[1][None])


def solution(mesh):
    spread = P("pipe", None, "ctx")
    return jax.shard_map(
        per_device,
        mesh=mesh,
        in_specs=(spread,) * 6 + (P("pipe", None),),
        out_specs=(spread,) * 4,
        check_vma=False,
    )
```

```python
import functools
import math

import jax
import jax.numpy as jnp
from jax import lax
from jax.experimental import pallas as pl
from jax.experimental.pallas import tpu as pltpu
from jax.sharding import PartitionSpec as P


def plus(a, b):
    return b if a is None else a if b is None else a + b


def minus(a, b):
    return a if b is None else -b if a is None else a - b


def turn(a, b, k, n):
    k = k % n
    if k == 0:
        return a, b
    if 4 * k == n:
        return b, minus(None, a)
    if 4 * k == 3 * n:
        return minus(None, b), a
    c, s = math.cos(2 * math.pi * k / n), math.sin(2 * math.pi * k / n)

    def scaled(v, f):
        return None if v is None else v * f

    if 8 * k == n:
        return scaled(plus(a, b), c), scaled(minus(b, a), c)
    return plus(scaled(a, c), scaled(b, s)), minus(scaled(b, c), scaled(a, s))


def real_dft(x, n):
    if n == 2:
        return [(x[0], None), (x[0], None)]
    even, odd = real_dft(x[0::2], n // 2), real_dft(x[1::2], n // 2)
    out = [None] * (n // 2 + 1)
    for k in range(n // 4 + 1):
        er, ei = even[k]
        tr, ti = turn(*odd[k], k, n)
        if 4 * k == n:
            out[k] = (plus(er, tr), plus(ei, ti))
        else:
            out[k] = (plus(er, tr), plus(ei, ti))
            out[n // 2 - k] = (minus(er, tr), minus(ti, ei))
    return out


def real_inverse(spec, n):
    if n == 2:
        return [plus(spec[0][0], spec[1][0])]
    even, odd = [], []
    for k in range(n // 4 + 1):
        xr, xi = spec[k]
        if 4 * k == n:
            even.append((xr + xr, None))
            odd.append((minus(None, None if xi is None else xi + xi), None))
            continue
        yr, yi = spec[n // 2 - k]
        even.append((plus(xr, yr), minus(xi, yi)))
        dr, di = minus(xr, yr), plus(xi, yi)
        odd.append(turn(dr, di, -k, n))
    even[0], odd[0] = (even[0][0], None), (odd[0][0], None)
    first, second = real_inverse(even, n // 2), real_inverse(odd, n // 2)
    return [v for pair in zip(first, second) for v in pair]


def make_tables(w, wi, twist):
    tokens = w.shape[0] // 2
    tiles = twist.shape[0] - 1
    j = lax.broadcasted_iota(jnp.int32, (tokens, tokens), 0)
    k = lax.broadcasted_iota(jnp.int32, (tokens, tokens), 1)
    phase = lax.rem(j * k, tokens).astype(jnp.float32) * (2.0 * math.pi / tokens)
    cb, sb = jnp.cos(phase).astype(jnp.bfloat16), jnp.sin(phase).astype(jnp.bfloat16)
    for ref, sign in ((w, -1.0), (wi, 1.0)):
        ref[0:tokens, 0:tokens] = cb
        ref[tokens : 2 * tokens, tokens : 2 * tokens] = cb
        ref[0:tokens, tokens : 2 * tokens] = sb * sign
        ref[tokens : 2 * tokens, 0:tokens] = sb * -sign
    lane = lax.broadcasted_iota(jnp.int32, (1, tokens), 1)
    unit = 2.0 * math.pi / (2 * tiles * tokens)

    def row(t, carry):
        angle = (lane * t).astype(jnp.float32) * unit
        twist[t, 0:1, :] = jnp.cos(angle)
        twist[t, 1:2, :] = jnp.sin(angle)
        return carry

    lax.fori_loop(0, tiles + 1, row, 0)


ROWS = 16
VMEM_MIB = 49


def transform(rx, out, w, wi, twist, spec, back):
    _, tiles, rows, tokens = rx.shape
    full = 2 * tiles * tokens
    shrink = 1.0 / math.sqrt(tiles * tokens)
    steps = rows // ROWS

    def first(t, carry):
        s, i = lax.div(t, steps), lax.rem(t, steps)
        at = pl.ds(pl.multiple_of(i * ROWS, ROWS), ROWS)
        x = [rx[s, a, at, :].astype(jnp.float32) for a in range(tiles)]
        for k, (re, im) in enumerate(real_dft(x, 2 * tiles)):
            if k == 0:
                new_re, new_im = re, jnp.zeros_like(re)
            else:
                c, d = twist[k, 0:1, :], twist[k, 1:2, :]
                new_re = plus(re * c, None if im is None else im * d)
                new_im = minus(None if im is None else im * c, re * d)
            spec[s, k, at, 0:tokens] = new_re.astype(jnp.bfloat16)
            spec[s, k, at, tokens : 2 * tokens] = new_im.astype(jnp.bfloat16)
        return carry

    lax.fori_loop(0, 3 * steps, first, 0)

    def middle(k, carry):
        def spectrum(s):
            u = jnp.dot(spec[s, k], w[...], preferred_element_type=jnp.float32)
            u = u.astype(jnp.bfloat16).astype(jnp.float32)
            return u[:, :tokens], u[:, tokens:]

        hr, hi = spectrum(0)
        zr, zi = spectrum(1)
        dr, di = spectrum(2)
        c = twist[k, 0:1, :] * (1.0 / full)
        d = twist[k, 1:2, :] * (1.0 / full)
        for s, (ur, ui, f) in enumerate(((hr, hi, 1.0), (zr, zi, shrink))):
            qr = ur * dr + ui * di
            qi = ur * di - ui * dr
            if s:
                qr, qi = qr * f, qi * f
            q = jnp.concatenate([qr, qi], axis=1).astype(jnp.bfloat16)
            e = jnp.dot(q, wi[...], preferred_element_type=jnp.float32)
            er, ei = e[:, :tokens], e[:, tokens:]
            back[s, k, :, 0:tokens] = (er * c - ei * d).astype(jnp.bfloat16)
            back[s, k, :, tokens : 2 * tokens] = (er * d + ei * c).astype(jnp.bfloat16)
        return carry

    lax.fori_loop(0, tiles + 1, middle, 0)

    def last(t, carry):
        s, i = lax.div(t, steps), lax.rem(t, steps)
        at = pl.ds(pl.multiple_of(i * ROWS, ROWS), ROWS)
        pieces = []
        for k in range(tiles + 1):
            re = back[s, k, at, 0:tokens].astype(jnp.float32)
            im = None
            if 0 < k < tiles:
                im = back[s, k, at, tokens : 2 * tokens].astype(jnp.float32)
            pieces.append((re, im))
        for a, value in enumerate(real_inverse(pieces, 2 * tiles)):
            out[s, a, at, :] = value.astype(jnp.bfloat16)
        return carry

    lax.fori_loop(0, 2 * steps, last, 0)


MESH = pl.DeviceIdType.MESH


def kernel(
    n, sections, group,
    arriving, taps, gate_in, inner_src, vals_src, saved_src, bias,
    gate_out, inner_out, vals_out, taps_out,
    gate, inner_in, vals, saved, w, wi, twist,
    grad, stage, rx, res, q, biased, spec, back,
    loads, pair_send, pair_recv, send, recv, home, back_send, back_recv, back_home,
):
    me, sec = lax.axis_index("ctx"), lax.axis_index("pipe")
    groups = arriving.shape[1] // group

    def rows_of(g):
        return pl.ds(pl.multiple_of(g * group, group), group)

    def peer_of(d):
        return lax.rem(me + d, n)

    def load(i):
        src = (inner_src, vals_src, gate_in, saved_src)[i]
        dst = (inner_in, vals, gate, saved)[i]
        return pltpu.make_async_copy(src, dst, loads.at[i])

    for i in range(4):
        load(i).start()
    barrier = pltpu.get_barrier_semaphore()
    pl.semaphore_signal(
        barrier, inc=1, device_id={"pipe": lax.rem(sec + 1, sections)}, device_id_type=MESH
    )

    def greet(d, carry):
        pl.semaphore_signal(barrier, inc=1, device_id={"ctx": peer_of(d)}, device_id_type=MESH)
        return carry

    lax.fori_loop(1, n, greet, 0)
    pl.semaphore_wait(barrier, n)

    def pair(g):
        return pltpu.make_async_remote_copy(
            src_ref=arriving.at[:, rows_of(g)],
            dst_ref=grad.at[:, rows_of(g)],
            send_sem=pair_send.at[g],
            recv_sem=pair_recv.at[g],
            device_id={"pipe": lax.rem(sec + sections - 1, sections)},
            device_id_type=MESH,
        )

    def start_pair(g, carry):
        pair(g).start()
        return carry

    lax.fori_loop(0, groups, start_pair, 0)

    def ship(src, g, s, p):
        pltpu.make_async_remote_copy(
            src_ref=src,
            dst_ref=rx.at[g, s, me],
            send_sem=send.at[g],
            recv_sem=recv.at[g],
            device_id={"ctx": p},
            device_id_type=MESH,
        ).start()

    def own_taps(g):
        return pltpu.make_async_copy(taps.at[me, rows_of(g)], rx.at[g, 0, me], home.at[g])

    def forward(g, carry):
        rows = rows_of(g)

        def send_taps(d, c):
            ship(taps.at[peer_of(d), rows], g, 0, peer_of(d))
            return c

        lax.fori_loop(1, n, send_taps, 0)
        own_taps(g).start()

        def product(left, right, s):
            def one(p):
                return (left[p, rows].astype(jnp.float32) * right[p, rows].astype(jnp.float32)).astype(
                    jnp.bfloat16
                )

            def make(d, c):
                stage[g, s - 1, peer_of(d)] = one(peer_of(d))
                return c

            lax.fori_loop(1, n, make, 0)
            rx[g, s, me] = one(me)

            def post(d, c):
                ship(stage.at[g, s - 1, peer_of(d)], g, s, peer_of(d))
                return c

            lax.fori_loop(1, n, post, 0)

        product(inner_in, vals, 1)
        pair(g).wait_recv()
        product(grad, gate, 2)
        return carry

    for i in range(3):
        load(i).wait()
    lax.fori_loop(0, groups, forward, 0)
    load(3).wait()
    make_tables(w, wi, twist)
    own, tokens = arriving.shape[1:]
    lanes = 128
    f32 = jnp.float32

    def side(b, carry):
        if own >= lanes:
            per = own // lanes
            at = (lax.div(b, per), pl.ds(pl.multiple_of(lax.rem(b, per) * lanes, lanes), lanes))
        else:
            at = (pl.ds(b * (lanes // own), lanes // own),)
        shape = grad[at].shape
        g = grad[at].astype(f32).reshape(lanes, tokens)
        gate_out[at] = (g * saved[at].astype(f32).reshape(lanes, tokens)).astype(
            jnp.bfloat16
        ).reshape(shape)
        d_out = (g * gate[at].astype(f32).reshape(lanes, tokens)).astype(jnp.bfloat16)
        row = bias[:, pl.ds(pl.multiple_of(b * lanes, lanes), lanes)]
        column = jnp.transpose(jnp.broadcast_to(row, (tokens, lanes)))
        biased[at] = (column * d_out.astype(f32)).reshape(shape)
        return carry

    lax.fori_loop(0, n * own // lanes, side, 0)

    def own_result(g):
        return pltpu.make_async_copy(
            res.at[g, :, me], q.at[g, :, me], back_home.at[g]
        )

    def turn_group(g, carry):
        landed = rx.at[g, :, pl.ds(0, n - 1)]
        pltpu.make_async_copy(landed, landed, recv.at[g]).wait()
        own_taps(g).wait()
        transform(rx.at[g], res.at[g], w, wi, twist, spec, back)

        def reply(d, c):
            pltpu.make_async_remote_copy(
                src_ref=res.at[g, :, peer_of(d)],
                dst_ref=q.at[g, :, me],
                send_sem=back_send.at[g],
                recv_sem=back_recv.at[g],
                device_id={"ctx": peer_of(d)},
                device_id_type=MESH,
            ).start()
            return c

        lax.fori_loop(1, n, reply, 0)
        own_result(g).start()
        return carry

    lax.fori_loop(0, groups, turn_group, 0)

    def finish(g, carry):
        rows = rows_of(g)
        replies = q.at[g, :, pl.ds(0, n - 1)]
        pltpu.make_async_copy(replies, replies, back_recv.at[g]).wait()
        own_result(g).wait()

        def product(p, c):
            dz = q[g, 0, p].astype(f32) + biased[p, rows]
            inner_out[p, rows] = (dz * vals[p, rows].astype(f32)).astype(jnp.bfloat16)
            vals_out[p, rows] = (dz * inner_in[p, rows].astype(f32)).astype(jnp.bfloat16)
            taps_out[p, rows] = q[g, 1, p]
            return c

        lax.fori_loop(0, n, product, 0)
        pair(g).wait_send()
        sent = rx.at[g, :, pl.ds(0, n - 1)]
        pltpu.make_async_copy(sent, sent, send.at[g]).wait()
        replied = res.at[g, :, pl.ds(0, n - 1)]
        pltpu.make_async_copy(replied, replied, back_send.at[g]).wait()
        return carry

    lax.fori_loop(0, groups, finish, 0)


def exchange(arriving, taps, gate, inner_in, vals, saved, bias, n, sections):
    _, own, tokens = arriving.shape
    group = max(ROWS, own // 4)
    groups = own // group
    bf16 = jnp.bfloat16
    vmem = pl.BlockSpec(memory_space=pltpu.VMEM)
    hbm = pl.BlockSpec(memory_space=pltpu.HBM)
    dma = pltpu.SemaphoreType.DMA
    whole = jax.ShapeDtypeStruct((n, own, tokens), bf16)
    held = pltpu.VMEM((n, own, tokens), bf16)
    return pl.pallas_call(
        functools.partial(kernel, n, sections, group),
        in_specs=[hbm] * 6 + [vmem],
        out_specs=[vmem] * 4,
        out_shape=[whole] * 4,
        scratch_shapes=[
            held, held, held, held,
            pltpu.VMEM((2 * tokens, 2 * tokens), bf16),
            pltpu.VMEM((2 * tokens, 2 * tokens), bf16),
            pltpu.VMEM((n + 1, 2, tokens), jnp.float32),
            held,
            pltpu.VMEM((groups, 2, n, group, tokens), bf16),
            pltpu.VMEM((groups, 3, n, group, tokens), bf16),
            pltpu.VMEM((groups, 2, n, group, tokens), bf16),
            pltpu.VMEM((groups, 2, n, group, tokens), bf16),
            pltpu.VMEM((n, own, tokens), jnp.float32),
            pltpu.VMEM((3, n + 1, group, 2 * tokens), bf16),
            pltpu.VMEM((2, n + 1, group, 2 * tokens), bf16),
            dma((4,)),
            dma((groups,)), dma((groups,)), dma((groups,)), dma((groups,)), dma((groups,)),
            dma((groups,)), dma((groups,)), dma((groups,)),
        ],
        compiler_params=pltpu.CompilerParams(
            collective_id=0, has_side_effects=True, vmem_limit_bytes=VMEM_MIB * 2**20
        ),
    )(arriving, taps, gate, inner_in, vals, saved, bias)


def write_out(a, b, c, narrow, a_out, b_out, c_out, wide_out, wide, sems):
    n = narrow.shape[0]
    part = max(1, n // 4)
    plain = [
        pltpu.make_async_copy(src, dst, sems.at[i])
        for i, (src, dst) in enumerate(((a, a_out), (b, b_out), (c, c_out)))
    ]
    for copy in plain:
        copy.start()
    widened = []
    for i in range(n // part):

        def widen(p, carry):
            wide[p] = narrow[p].astype(jnp.float32)
            return carry

        lax.fori_loop(i * part, (i + 1) * part, widen, 0)
        at = pl.ds(i * part, part)
        copy = pltpu.make_async_copy(wide.at[at], wide_out.at[at], sems.at[3 + i])
        copy.start()
        widened.append(copy)
    for copy in plain + widened:
        copy.wait()


def finish_outputs(d_gate, inner_gradient, d_values, d_filters):
    shape = d_gate.shape
    vmem = pl.BlockSpec(memory_space=pltpu.VMEM)
    hbm = pl.BlockSpec(memory_space=pl.ANY)
    narrow = jax.ShapeDtypeStruct(shape, jnp.bfloat16)
    return pl.pallas_call(
        write_out,
        in_specs=[vmem] * 4,
        out_specs=[hbm] * 4,
        out_shape=[narrow] * 3 + [jax.ShapeDtypeStruct(shape, jnp.float32)],
        scratch_shapes=[
            pltpu.VMEM(shape, jnp.float32),
            pltpu.SemaphoreType.DMA((3 + shape[0] // max(1, shape[0] // 4),)),
        ],
        compiler_params=pltpu.CompilerParams(vmem_limit_bytes=VMEM_MIB * 2**20),
    )(d_gate, inner_gradient, d_values, d_filters)


def per_device(arriving, input_gate, input_inner, values, conv_out, filters, bias):
    tiles = lax.axis_size("ctx")
    sections = lax.axis_size("pipe")
    channels, tokens = values.shape[1:]
    own = channels // tiles

    def split(array):
        return array[0].reshape(tiles, own, tokens)

    outs = exchange(
        split(arriving), split(filters), split(input_gate), split(input_inner), split(values),
        split(conv_out), bias, tiles, sections,
    )
    return tuple(array.reshape(1, channels, tokens) for array in finish_outputs(*outs))


def solution(mesh):
    spread = P("pipe", None, "ctx")
    return jax.shard_map(
        per_device,
        mesh=mesh,
        in_specs=(spread,) * 6 + (P("pipe", None),),
        out_specs=(spread,) * 4,
        check_vma=False,
    )
```
